32 devices in a mesh: fsdp: 32 (over z, y, x, core).
Axes of the slice: x: 2, y: 2, z: 4, core: 2. Of those that a mesh axis runs over, the one named last changes fastest.
Arguments:
- latents: bfloat16 [128, 256, 384], P('fsdp'), may hold values from -6 to 6
- condition: bfloat16 [128, 384], P('fsdp'), may hold values from -6 to 6
- modulation_weight: bfloat16 [884736], P('fsdp'), may hold values from -0.3125 to 0.3125
- input_weight: bfloat16 [442368], P('fsdp'), may hold values from -0.3125 to 0.3125
- output_weight: bfloat16 [147456], P('fsdp'), may hold values from -3.5 to 3.5
- first_weight: bfloat16 [589824], P('fsdp'), may hold values from -0.3125 to 0.3125
- second_weight: bfloat16 [589824], P('fsdp'), may hold values from -0.3125 to 0.3125
- all_biases: bfloat16 [5376], P('fsdp'), may hold values from -3 to 3
- cotangent: bfloat16 [128, 256, 384], P('fsdp'), may hold values from -6 to 6
Outputs:
- block_output: bfloat16 [128, 256, 384], P('fsdp')
- grad_latents: float32 [128, 256, 384], P('fsdp')
- grad_condition: float32 [128, 384], P('fsdp')
- grad_modulation: float32 [884736], P('fsdp')
- grad_input_weight: float32 [442368], P('fsdp')
- grad_output_weight: float32 [147456], P('fsdp')
- grad_first: float32 [589824], P('fsdp')
- grad_second: float32 [589824], P('fsdp')
- grad_biases: float32 [5376], P('fsdp')
The draws below stay inside these ranges and needn't reach their ends.
All inputs are finite; a program needn't handle non-finite values.
Results may differ from the reference program's by a relative error of at most 0.01.
The reference program's roundings to bfloat16 on the way count: a program that leaves them out, or rounds other values in their place, can miss the bound.
Values may be sent and summed in bfloat16 or wider, within the bound.
A program may use at most 128 MiB of HBM per device.

```python
import math
import jax
import jax.numpy as jnp
from jax import lax

D = 384
HEADS = 6
HDIM = 64
FF = 1536
SEQ = 256
LATENTS = 128


def shard_levels(own_key, dims, shards, least, top_value):
    loudness = 1.0
    for dim, blocks in shards:
        heights = jax.random.uniform(jax.random.fold_in(jax.random.fold_in(own_key, 6), dim), (blocks,), jnp.float32, least / len(shards), top_value / len(shards))
        loudness = loudness * jnp.repeat(jnp.exp(heights), dims[dim] // blocks).reshape((-1,) + (1,) * (len(dims) - 1 - dim))
    return loudness


def centred(own_key, shape, width, limit, shards=(), dtype=jnp.bfloat16):
    entries = width * jax.random.normal(own_key, shape, jnp.float32)
    if shards:
        entries = entries * shard_levels(own_key, shape, shards, -0.22, 0.18)
    return jnp.clip(entries, -limit, limit).astype(dtype)


def setup_inputs(seed: int = 0) -> dict:
    seeds = jax.random.split(jax.random.key(seed), 10)
    latents = centred(seeds[0], (LATENTS, SEQ, D), 1.0, 6.0, ((0, 32),))
    condition = centred(seeds[1], (LATENTS, D), 1.0, 6.0, ((0, 32),))
    modulation_weight = centred(seeds[2], (6 * D * D,), D ** -0.5, 0.3125, ((0, 32),))
    input_weight = centred(seeds[3], (3 * D * D,), D ** -0.5, 0.3125, ((0, 32),))
    output_weight = centred(seeds[4], (D * D,), (max(D // 128, 1)) ** -0.5, 3.5, ((0, 32),))
    first_weight = centred(seeds[5], (D * FF,), D ** -0.5, 0.3125, ((0, 32),))
    second_weight = centred(seeds[6], (FF * D,), (FF // 4) ** -0.5, 0.3125, ((0, 32),))
    all_biases = centred(seeds[7], (10 * D + FF,), 0.5, 3.0, ((0, 32),))
    cotangent = centred(seeds[8], (LATENTS, SEQ, D), 1.0, 6.0, ((0, 32),))
    return {"latents": latents, "condition": condition, "modulation_weight": modulation_weight, "input_weight": input_weight, "output_weight": output_weight, "first_weight": first_weight, "second_weight": second_weight, "all_biases": all_biases, "cotangent": cotangent}


EPSILON = 1e-06

def product(left, right):
    return jnp.dot(left, right, preferred_element_type=jnp.float32)

def outer_sum(left, right):
    return product(left.reshape(-1, left.shape[-1]).T, right.reshape(-1, right.shape[-1]))

def batched(form, left, right):
    return jnp.einsum(form, left.astype(jnp.float32), right.astype(jnp.float32))

def normalize(inputs):
    average = lax.optimization_barrier(jnp.mean(inputs, axis=-1, keepdims=True))
    centered = inputs - average
    inv_std = lax.rsqrt(lax.optimization_barrier(jnp.mean(centered * centered, axis=-1, keepdims=True)) + EPSILON)
    return (centered * inv_std, inv_std)

def normalize_back(grad_normed, normed, inv_std):
    first_mean = lax.optimization_barrier(jnp.mean(grad_normed, axis=-1, keepdims=True))
    second_mean = lax.optimization_barrier(jnp.mean(grad_normed * normed, axis=-1, keepdims=True))
    return inv_std * (grad_normed - first_mean - normed * second_mean)

def gelu_tanh(inputs):
    return jax.nn.gelu(inputs, approximate=True)

def split_heads(tensor):
    return tensor.reshape(tensor.shape[0], tensor.shape[1], HEADS, HDIM)

def unpack(flat_mod, flat_input, flat_output, flat_first, flat_second, bias_flat, model_width, hidden):
    bias_float = bias_flat.astype(jnp.float32)
    return {'mod': flat_mod.reshape(model_width, 6 * model_width), 'inproj': flat_input.reshape(model_width, 3 * model_width), 'outproj': flat_output.reshape(model_width, model_width), 'first': flat_first.reshape(model_width, hidden), 'second': flat_second.reshape(hidden, model_width), 'bias_mod': bias_float[:6 * model_width], 'bias_query': bias_float[6 * model_width:7 * model_width], 'bias_value': bias_float[7 * model_width:8 * model_width], 'bias_outproj': bias_float[8 * model_width:9 * model_width], 'bias_first': bias_float[9 * model_width:9 * model_width + hidden], 'bias_second': bias_float[9 * model_width + hidden:]}

def forward_pass(latents, condition, params, einsum_fn):
    model_width = latents.shape[-1]
    score_scale = 1.0 / math.sqrt(HDIM)
    cond_float = condition.astype(jnp.float32)
    cond_act = jax.nn.silu(cond_float).astype(jnp.bfloat16)
    modulation = product(cond_act, params['mod']) + params['bias_mod']
    mod_parts = [modulation[:, None, piece_index * model_width:(piece_index + 1) * model_width] for piece_index in range(6)]
    inputs = latents.astype(jnp.float32)
    normed_one, inv_one = normalize(inputs)
    modul_one = (normed_one * (1.0 + mod_parts[1]) + mod_parts[0]).astype(jnp.bfloat16)
    projected = product(modul_one, params['inproj'])
    queries = (projected[..., :model_width] + params['bias_query']).astype(jnp.bfloat16)
    key_rows = projected[..., model_width:2 * model_width].astype(jnp.bfloat16)
    value_rows = (projected[..., 2 * model_width:] + params['bias_value']).astype(jnp.bfloat16)
    scores = einsum_fn('lqhd,lkhd->lhqk', split_heads(queries), split_heads(key_rows)) * score_scale
    row_max = lax.optimization_barrier(jnp.max(scores, axis=-1, keepdims=True))
    log_total = row_max + jnp.log(lax.optimization_barrier(jnp.sum(jnp.exp(scores - row_max), axis=-1, keepdims=True)))
    probabilities = jnp.exp(scores - log_total).astype(jnp.bfloat16)
    attended = einsum_fn('lhqk,lkhd->lqhd', probabilities, split_heads(value_rows))
    attended = attended.reshape(latents.shape).astype(jnp.bfloat16)
    branch_one = product(attended, params['outproj']) + params['bias_outproj']
    middle = inputs + mod_parts[2] * branch_one
    normed_two, inv_two = normalize(middle)
    modul_two = (normed_two * (1.0 + mod_parts[4]) + mod_parts[3]).astype(jnp.bfloat16)
    pre_act = product(modul_two, params['first']) + params['bias_first']
    activated = gelu_tanh(pre_act).astype(jnp.bfloat16)
    branch_two = product(activated, params['second']) + params['bias_second']
    block_output = (middle + mod_parts[5] * branch_two).astype(jnp.bfloat16)
    saved_state = {'cond_float': cond_float, 'cond_act': cond_act, 'mod_parts': mod_parts, 'normed_one': normed_one, 'inv_one': inv_one, 'modul_one': modul_one, 'queries': queries, 'key_rows': key_rows, 'value_rows': value_rows, 'log_total': log_total, 'attended': attended, 'branch_one': branch_one, 'normed_two': normed_two, 'inv_two': inv_two, 'modul_two': modul_two, 'pre_act': pre_act, 'activated': activated, 'branch_two': branch_two}
    return (block_output, saved_state)

def backward_feed(cotangent, saved_state, params, einsum_fn):
    mod_parts = saved_state['mod_parts']
    upstream = cotangent.astype(jnp.float32)
    grad_gate_two = lax.optimization_barrier(jnp.sum(upstream * saved_state['branch_two'], axis=1))
    grad_branch = upstream * mod_parts[5]
    branch_round = grad_branch.astype(jnp.bfloat16)
    grad_second = outer_sum(saved_state['activated'], branch_round)
    bias_second = lax.optimization_barrier(jnp.sum(grad_branch, axis=(0, 1)))
    grad_act = product(branch_round, params['second'].T)
    grad_pre = jax.vjp(gelu_tanh, saved_state['pre_act'])[1](grad_act)[0]
    pre_round = grad_pre.astype(jnp.bfloat16)
    grad_first = outer_sum(saved_state['modul_two'], pre_round)
    bias_first = lax.optimization_barrier(jnp.sum(grad_pre, axis=(0, 1)))
    grad_modul = product(pre_round, params['first'].T)
    grad_shift_two = lax.optimization_barrier(jnp.sum(grad_modul, axis=1))
    grad_scale_two = lax.optimization_barrier(jnp.sum(grad_modul * saved_state['normed_two'], axis=1))
    grad_middle = upstream + normalize_back(grad_modul * (1.0 + mod_parts[4]), saved_state['normed_two'], saved_state['inv_two'])
    mods_two = (grad_shift_two, grad_scale_two, grad_gate_two)
    return (grad_middle, mods_two, grad_first, grad_second, bias_first, bias_second)

def backward_attention(grad_middle, mods_two, saved_state, params, einsum_fn):
    mod_parts = saved_state['mod_parts']
    score_scale = 1.0 / math.sqrt(HDIM)
    grad_gate_one = lax.optimization_barrier(jnp.sum(grad_middle * saved_state['branch_one'], axis=1))
    grad_branch = grad_middle * mod_parts[2]
    branch_round = grad_branch.astype(jnp.bfloat16)
    grad_outproj = outer_sum(saved_state['attended'], branch_round)
    bias_outproj = lax.optimization_barrier(jnp.sum(grad_branch, axis=(0, 1)))
    grad_attended = product(branch_round, params['outproj'].T).astype(jnp.bfloat16)
    query_heads = split_heads(saved_state['queries'])
    key_heads = split_heads(saved_state['key_rows'])
    value_heads = split_heads(saved_state['value_rows'])
    attended_heads = split_heads(grad_attended)
    scores = einsum_fn('lqhd,lkhd->lhqk', query_heads, key_heads) * score_scale
    prob_float = jnp.exp(scores - saved_state['log_total'])
    prob_round = prob_float.astype(jnp.bfloat16)
    grad_probs = einsum_fn('lqhd,lkhd->lhqk', attended_heads, value_heads)
    row_dots = lax.optimization_barrier(jnp.sum(prob_float * grad_probs, axis=-1, keepdims=True))
    grad_scores = (prob_float * (grad_probs - row_dots) * score_scale).astype(jnp.bfloat16)
    grad_query = einsum_fn('lhqk,lkhd->lqhd', grad_scores, key_heads).reshape(grad_middle.shape)
    grad_key = einsum_fn('lhqk,lqhd->lkhd', grad_scores, query_heads).reshape(grad_middle.shape)
    grad_value = einsum_fn('lhqk,lqhd->lkhd', prob_round, attended_heads).reshape(grad_middle.shape)
    bias_query = lax.optimization_barrier(jnp.sum(grad_query, axis=(0, 1)))
    bias_value = lax.optimization_barrier(jnp.sum(grad_value, axis=(0, 1)))
    grad_proj = jnp.concatenate([grad_query, grad_key, grad_value], axis=-1).astype(jnp.bfloat16)
    grad_inproj = outer_sum(saved_state['modul_one'], grad_proj)
    grad_modul = product(grad_proj, params['inproj'].T)
    grad_shift_one = lax.optimization_barrier(jnp.sum(grad_modul, axis=1))
    grad_scale_one = lax.optimization_barrier(jnp.sum(grad_modul * saved_state['normed_one'], axis=1))
    grad_latents = grad_middle + normalize_back(grad_modul * (1.0 + mod_parts[1]), saved_state['normed_one'], saved_state['inv_one'])
    grad_mod = jnp.concatenate([grad_shift_one, grad_scale_one, grad_gate_one, mods_two[0], mods_two[1], mods_two[2]], axis=-1)
    mod_round = grad_mod.astype(jnp.bfloat16)
    grad_modw = product(saved_state['cond_act'].T, mod_round)
    bias_mod = lax.optimization_barrier(jnp.sum(grad_mod, axis=0))
    grad_cond_act = product(mod_round, params['mod'].T)
    grad_condition = jax.vjp(jax.nn.silu, saved_state['cond_float'])[1](grad_cond_act)[0]
    biases_head = (bias_mod, bias_query, bias_value, bias_outproj)
    return (grad_latents, grad_condition, grad_modw, grad_inproj, grad_outproj, biases_head)

def reference(latents, condition, modulation_weight, input_weight, output_weight, first_weight, second_weight, all_biases, cotangent):
    params = unpack(modulation_weight, input_weight, output_weight, first_weight, second_weight, all_biases, D, FF)
    block_size = 16 if LATENTS % 16 == 0 else 1
    block_count = LATENTS // block_size

    def block_step(running, pieces):
        lat_block, cond_block, cot_block = pieces
        block_output, saved_state = forward_pass(lat_block, cond_block, params, batched)
        grad_middle, mods_two, grad_first, grad_second, bias_first, bias_second = backward_feed(cot_block, saved_state, params, batched)
        grad_lat, grad_cond, grad_modw, grad_inproj, grad_outproj, biases_head = backward_attention(grad_middle, mods_two, saved_state, params, batched)
        bias_vector = jnp.concatenate([biases_head[0], biases_head[1], biases_head[2], biases_head[3], bias_first, bias_second])
        updated = (running[0] + grad_modw, running[1] + grad_inproj, running[2] + grad_outproj, running[3] + grad_first, running[4] + grad_second, running[5] + bias_vector)
        return (updated, (block_output, grad_lat, grad_cond))
    initial = (jnp.zeros((D, 6 * D), jnp.float32), jnp.zeros((D, 3 * D), jnp.float32), jnp.zeros((D, D), jnp.float32), jnp.zeros((D, FF), jnp.float32), jnp.zeros((FF, D), jnp.float32), jnp.zeros((10 * D + FF,), jnp.float32))
    totals, results = lax.scan(block_step, initial, (latents.reshape(block_count, block_size, SEQ, D), condition.reshape(block_count, block_size, D), cotangent.reshape(block_count, block_size, SEQ, D)))
    block_output = results[0].reshape(LATENTS, SEQ, D)
    grad_latents = results[1].reshape(LATENTS, SEQ, D)
    grad_condition = results[2].reshape(LATENTS, D)
    return (block_output, grad_latents, grad_condition, totals[0].reshape(-1), totals[1].reshape(-1), totals[2].reshape(-1), totals[3].reshape(-1), totals[4].reshape(-1), totals[5])
```

```python
import functools
import math

import jax
import jax.numpy as jnp
from jax import lax
from jax.experimental import pallas as pl
from jax.experimental.pallas import tpu as pltpu
from jax.sharding import PartitionSpec as P

HEADS = 6
HDIM = 64
FF = 1536


EPSILON = 1e-06


def product(left, right):
    return jnp.dot(left, right, preferred_element_type=jnp.float32)


def outer_sum(left, right):
    return product(left.reshape(-1, left.shape[-1]).T, right.reshape(-1, right.shape[-1]))


def batched(form, left, right):
    return jnp.einsum(form, left, right, preferred_element_type=jnp.float32)


def normalize(inputs):
    average = jnp.mean(inputs, axis=-1, keepdims=True)
    centered = inputs - average
    inv_std = lax.rsqrt(jnp.mean(centered * centered, axis=-1, keepdims=True) + EPSILON)
    return (centered * inv_std, inv_std)


def normalize_back(grad_normed, normed, inv_std):
    first_mean = jnp.mean(grad_normed, axis=-1, keepdims=True)
    second_mean = jnp.mean(grad_normed * normed, axis=-1, keepdims=True)
    return inv_std * (grad_normed - first_mean - normed * second_mean)


def gelu_tanh(inputs):
    return jax.nn.gelu(inputs, approximate=True)


def split_heads(tensor):
    return tensor.reshape(tensor.shape[0], tensor.shape[1], HEADS, HDIM)


def unpack(
    flat_mod, flat_input, flat_output, flat_first, flat_second, bias_flat, model_width, hidden
):
    bias_float = bias_flat.astype(jnp.float32)
    return {
        "mod": flat_mod.reshape(model_width, 6 * model_width),
        "inproj": flat_input.reshape(model_width, 3 * model_width),
        "outproj": flat_output.reshape(model_width, model_width),
        "first": flat_first.reshape(model_width, hidden),
        "second": flat_second.reshape(hidden, model_width),
        "bias_mod": bias_float[: 6 * model_width],
        "bias_query": bias_float[6 * model_width : 7 * model_width],
        "bias_value": bias_float[7 * model_width : 8 * model_width],
        "bias_outproj": bias_float[8 * model_width : 9 * model_width],
        "bias_first": bias_float[9 * model_width : 9 * model_width + hidden],
        "bias_second": bias_float[9 * model_width + hidden :],
    }


def forward_pass(latents, condition, params, einsum_fn):
    model_width = latents.shape[-1]
    score_scale = 1.0 / math.sqrt(HDIM)
    cond_float = condition.astype(jnp.float32)
    cond_act = jax.nn.silu(cond_float).astype(jnp.bfloat16)
    modulation = product(cond_act, params["mod"]) + params["bias_mod"]
    mod_parts = [
        modulation[:, None, piece_index * model_width : (piece_index + 1) * model_width]
        for piece_index in range(6)
    ]
    inputs = latents.astype(jnp.float32)
    normed_one, inv_one = normalize(inputs)
    modul_one = (normed_one * (1.0 + mod_parts[1]) + mod_parts[0]).astype(jnp.bfloat16)
    projected = product(modul_one, params["inproj"])
    queries = (projected[..., :model_width] + params["bias_query"]).astype(jnp.bfloat16)
    key_rows = projected[..., model_width : 2 * model_width].astype(jnp.bfloat16)
    value_rows = (projected[..., 2 * model_width :] + params["bias_value"]).astype(jnp.bfloat16)
    scores = einsum_fn("lqhd,lkhd->lhqk", split_heads(queries), split_heads(key_rows)) * score_scale
    row_max = jnp.max(scores, axis=-1, keepdims=True)
    log_total = row_max + jnp.log(jnp.sum(jnp.exp(scores - row_max), axis=-1, keepdims=True))
    probabilities = jnp.exp(scores - log_total).astype(jnp.bfloat16)
    attended = einsum_fn("lhqk,lkhd->lqhd", probabilities, split_heads(value_rows))
    attended = attended.reshape(latents.shape).astype(jnp.bfloat16)
    branch_one = product(attended, params["outproj"]) + params["bias_outproj"]
    middle = inputs + mod_parts[2] * branch_one
    normed_two, inv_two = normalize(middle)
    modul_two = (normed_two * (1.0 + mod_parts[4]) + mod_parts[3]).astype(jnp.bfloat16)
    pre_act = product(modul_two, params["first"]) + params["bias_first"]
    activated = gelu_tanh(pre_act).astype(jnp.bfloat16)
    branch_two = product(activated, params["second"]) + params["bias_second"]
    block_output = (middle + mod_parts[5] * branch_two).astype(jnp.bfloat16)
    saved_state = {
        "cond_float": cond_float,
        "cond_act": cond_act,
        "mod_parts": mod_parts,
        "normed_one": normed_one,
        "inv_one": inv_one,
        "modul_one": modul_one,
        "queries": queries,
        "key_rows": key_rows,
        "value_rows": value_rows,
        "log_total": log_total,
        "attended": attended,
        "branch_one": branch_one,
        "normed_two": normed_two,
        "inv_two": inv_two,
        "modul_two": modul_two,
        "pre_act": pre_act,
        "activated": activated,
        "branch_two": branch_two,
    }
    return (block_output, saved_state)


def backward_feed(cotangent, saved_state, params):
    mod_parts = saved_state["mod_parts"]
    upstream = cotangent.astype(jnp.float32)
    grad_gate_two = jnp.sum(upstream * saved_state["branch_two"], axis=1)
    grad_branch = upstream * mod_parts[5]
    branch_round = grad_branch.astype(jnp.bfloat16)
    grad_second = outer_sum(saved_state["activated"], branch_round)
    bias_second = jnp.sum(grad_branch, axis=(0, 1))
    grad_act = product(branch_round, params["second"].T)
    grad_pre = jax.vjp(gelu_tanh, saved_state["pre_act"])[1](grad_act)[0]
    pre_round = grad_pre.astype(jnp.bfloat16)
    grad_first = outer_sum(saved_state["modul_two"], pre_round)
    bias_first = jnp.sum(grad_pre, axis=(0, 1))
    grad_modul = product(pre_round, params["first"].T)
    grad_shift_two = jnp.sum(grad_modul, axis=1)
    grad_scale_two = jnp.sum(grad_modul * saved_state["normed_two"], axis=1)
    grad_middle = upstream + normalize_back(
        grad_modul * (1.0 + mod_parts[4]), saved_state["normed_two"], saved_state["inv_two"]
    )
    mods_two = (grad_shift_two, grad_scale_two, grad_gate_two)
    return (grad_middle, mods_two, grad_first, grad_second, bias_first, bias_second)


def backward_attention(grad_middle, mods_two, saved_state, params, einsum_fn):
    mod_parts = saved_state["mod_parts"]
    score_scale = 1.0 / math.sqrt(HDIM)
    grad_gate_one = jnp.sum(grad_middle * saved_state["branch_one"], axis=1)
    grad_branch = grad_middle * mod_parts[2]
    branch_round = grad_branch.astype(jnp.bfloat16)
    grad_outproj = outer_sum(saved_state["attended"], branch_round)
    bias_outproj = jnp.sum(grad_branch, axis=(0, 1))
    grad_attended = product(branch_round, params["outproj"].T).astype(jnp.bfloat16)
    query_heads = split_heads(saved_state["queries"])
    key_heads = split_heads(saved_state["key_rows"])
    value_heads = split_heads(saved_state["value_rows"])
    attended_heads = split_heads(grad_attended)
    scores = einsum_fn("lqhd,lkhd->lhqk", query_heads, key_heads) * score_scale
    prob_float = jnp.exp(scores - saved_state["log_total"])
    prob_round = prob_float.astype(jnp.bfloat16)
    grad_probs = einsum_fn("lqhd,lkhd->lhqk", attended_heads, value_heads)
    row_dots = jnp.sum(prob_float * grad_probs, axis=-1, keepdims=True)
    grad_scores = (prob_float * (grad_probs - row_dots) * score_scale).astype(jnp.bfloat16)
    grad_query = einsum_fn("lhqk,lkhd->lqhd", grad_scores, key_heads).reshape(grad_middle.shape)
    grad_key = einsum_fn("lhqk,lqhd->lkhd", grad_scores, query_heads).reshape(grad_middle.shape)
    grad_value = einsum_fn("lhqk,lqhd->lkhd", prob_round, attended_heads).reshape(grad_middle.shape)
    bias_query = jnp.sum(grad_query, axis=(0, 1))
    bias_value = jnp.sum(grad_value, axis=(0, 1))
    grad_proj = jnp.concatenate([grad_query, grad_key, grad_value], axis=-1).astype(jnp.bfloat16)
    grad_inproj = outer_sum(saved_state["modul_one"], grad_proj)
    grad_modul = product(grad_proj, params["inproj"].T)
    grad_shift_one = jnp.sum(grad_modul, axis=1)
    grad_scale_one = jnp.sum(grad_modul * saved_state["normed_one"], axis=1)
    grad_latents = grad_middle + normalize_back(
        grad_modul * (1.0 + mod_parts[1]), saved_state["normed_one"], saved_state["inv_one"]
    )
    grad_mod = jnp.concatenate(
        [grad_shift_one, grad_scale_one, grad_gate_one, mods_two[0], mods_two[1], mods_two[2]],
        axis=-1,
    )
    mod_round = grad_mod.astype(jnp.bfloat16)
    grad_modw = product(saved_state["cond_act"].T, mod_round)
    bias_mod = jnp.sum(grad_mod, axis=0)
    grad_cond_act = product(mod_round, params["mod"].T)
    grad_condition = jax.vjp(jax.nn.silu, saved_state["cond_float"])[1](grad_cond_act)[0]
    biases_head = (bias_mod, bias_query, bias_value, bias_outproj)
    return (grad_latents, grad_condition, grad_modw, grad_inproj, grad_outproj, biases_head)


MESH = pl.DeviceIdType.MESH
LANES = 128
ROW_TILE = 16


def slice_shape(devices):
    chips = devices // 2
    edge = 1
    while (2 * edge) ** 3 <= chips:
        edge *= 2
    return (chips // (edge * edge), edge, edge, 2)


def position(sizes):
    size_z, size_y, size_x, size_c = sizes
    me = lax.axis_index("fsdp")
    core = lax.rem(me, size_c)
    chip = me // size_c
    at_x = lax.rem(chip, size_x)
    at_y = lax.rem(chip // size_x, size_y)
    at_z = chip // (size_x * size_y)
    return (at_z, at_y, at_x, core)


def device_at(sizes, at):
    return ((at[0] * sizes[1] + at[1]) * sizes[2] + at[2]) * sizes[3] + at[3]


def moved(sizes, at, axis, step):
    at = list(at)
    at[axis] = lax.rem(at[axis] + step, sizes[axis])
    return tuple(at)


def enter(sizes, at):
    barrier = pltpu.get_barrier_semaphore()
    total = 0
    for axis in range(4):
        for step in range(1, sizes[axis]):
            peer = device_at(sizes, moved(sizes, at, axis, step))
            pl.semaphore_signal(barrier, inc=1, device_id=(peer,), device_id_type=MESH)
            total += 1
    pl.semaphore_wait(barrier, total)


def gather_kernel(sizes, cut, shard_ref, full_ref, own_sem, send_sem, recv_sem, core_send, core_recv):
    at = position(sizes)
    at_z, at_y, at_x, core = at
    rows = shard_ref.shape[0]
    upper, lower = pl.ds(0, cut), pl.ds(cut, rows - cut)
    enter(sizes, at)
    links, cores = [], []

    def send(source, target, axis, step):
        slot = len(links)
        copy = pltpu.make_async_remote_copy(
            src_ref=source,
            dst_ref=target,
            send_sem=send_sem.at[slot],
            recv_sem=recv_sem.at[slot],
            device_id=(device_at(sizes, moved(sizes, at, axis, step)),),
            device_id_type=MESH,
        )
        copy.start()
        links.append(copy)
        return copy

    def share(source, target):
        slot = len(cores)
        copy = pltpu.make_async_remote_copy(
            src_ref=source,
            dst_ref=target,
            send_sem=core_send.at[slot],
            recv_sem=core_recv.at[slot],
            device_id=(device_at(sizes, moved(sizes, at, 3, 1)),),
            device_id_type=MESH,
        )
        copy.start()
        cores.append(copy)

    mine = full_ref.at[at_z, at_y, at_x, core]
    first = [send(shard_ref, mine, 0, step) for step in range(1, sizes[0])]
    share(shard_ref, mine)
    own = pltpu.make_async_copy(shard_ref, mine, own_sem)
    own.start()
    own.wait()
    for copy in first:
        copy.wait_recv()
    along_y, along_x = [], []
    column = full_ref.at[:, at_y, at_x, core, upper]
    for step in range(1, sizes[1]):
        along_y.append(send(column, column, 1, step))
    column = full_ref.at[:, at_y, at_x, core, lower]
    for step in range(1, sizes[2]):
        along_x.append(send(column, column, 2, step))
    for step in range(1, sizes[0]):
        piece = full_ref.at[lax.rem(at_z + sizes[0] - step, sizes[0]), at_y, at_x, core]
        share(piece, piece)
    for copy in along_y:
        copy.wait_recv()
    last_x, last_y = [], []
    plane = full_ref.at[:, :, at_x, core, upper]
    for step in range(1, sizes[2]):
        last_x.append(send(plane, plane, 2, step))
    for copy in along_x:
        copy.wait_recv()
    plane = full_ref.at[:, at_y, :, core, lower]
    for step in range(1, sizes[1]):
        last_y.append(send(plane, plane, 1, step))
    for step in range(1, sizes[1]):
        piece = full_ref.at[:, lax.rem(at_y + sizes[1] - step, sizes[1]), at_x, core, upper]
        share(piece, piece)
    for step in range(1, sizes[2]):
        piece = full_ref.at[:, at_y, lax.rem(at_x + sizes[2] - step, sizes[2]), core, lower]
        share(piece, piece)
    for step, copy in enumerate(last_x, 1):
        copy.wait_recv()
        piece = full_ref.at[:, :, lax.rem(at_x + sizes[2] - step, sizes[2]), core, upper]
        share(piece, piece)
    for step, copy in enumerate(last_y, 1):
        copy.wait_recv()
        piece = full_ref.at[:, lax.rem(at_y + sizes[1] - step, sizes[1]), :, core, lower]
        share(piece, piece)
    for copy in links:
        copy.wait_send()
    for copy in cores:
        copy.wait()


def gather_all(shard, sizes):
    rows = shard.shape[0]
    cut = (rows // ROW_TILE + 1) // 2 * ROW_TILE
    link_count = (sizes[0] - 1) + 2 * (sizes[1] - 1) + 2 * (sizes[2] - 1)
    core_count = link_count + 1
    return pl.pallas_call(
        functools.partial(gather_kernel, sizes, cut),
        out_shape=jax.ShapeDtypeStruct(tuple(sizes) + shard.shape, shard.dtype),
        in_specs=[pl.BlockSpec(memory_space=pl.ANY)],
        out_specs=pl.BlockSpec(memory_space=pl.ANY),
        scratch_shapes=[
            pltpu.SemaphoreType.DMA,
            pltpu.SemaphoreType.DMA((link_count,)),
            pltpu.SemaphoreType.DMA((link_count,)),
            pltpu.SemaphoreType.DMA((core_count,)),
            pltpu.SemaphoreType.DMA((core_count,)),
        ],
        compiler_params=pltpu.CompilerParams(collective_id=0, has_side_effects=True),
    )(shard)


def scatter_kernel(
    sizes,
    cut,
    terms_ref,
    out_ref,
    pair_ref,
    upper_two,
    lower_two,
    upper_three,
    lower_three,
    last_ref,
    core_send,
    core_recv,
    send_sem,
    recv_sem,
):
    size_z, size_y, size_x = sizes[:3]
    at = position(sizes)
    at_z, at_y, at_x, core = at
    rows = out_ref.shape[0]
    upper, lower = pl.ds(0, cut), pl.ds(cut, rows - cut)
    links = []
    enter(sizes, at)

    def send(source, target, axis, step):
        slot = len(links)
        copy = pltpu.make_async_remote_copy(
            src_ref=source,
            dst_ref=target,
            send_sem=send_sem.at[slot],
            recv_sem=recv_sem.at[slot],
            device_id=(device_at(sizes, moved(sizes, at, axis, step)),),
            device_id_type=MESH,
        )
        copy.start()
        links.append(copy)
        return copy

    def near(size, place, step):
        return lax.rem(place + step, size)

    other = 1 - core
    pairs = []
    pieces = [("x", step) for step in range(1, size_x)] + [("y", step) for step in range(1, size_y)]
    pieces += [("x", 0), ("y", 0)]
    for slot, (way, step) in enumerate(pieces):
        if way == "x":
            to = near(size_x, at_x, step)
            source = terms_ref.at[:, :, to, other, upper]
            target = pair_ref.at[:, :, to, upper]
        else:
            to = near(size_y, at_y, step)
            source = terms_ref.at[:, to, :, other, lower]
            target = pair_ref.at[:, to, :, lower]
        copy = pltpu.make_async_remote_copy(
            src_ref=source,
            dst_ref=target,
            send_sem=core_send.at[slot],
            recv_sem=core_recv.at[slot],
            device_id=(device_at(sizes, moved(sizes, at, 3, 1)),),
            device_id_type=MESH,
        )
        copy.start()
        pairs.append(copy)

    def add_pair(way, step):
        if way == "x":
            to = near(size_x, at_x, step)

            @pl.loop(0, size_z * size_y)
            def _(index):
                z, y = index // size_y, lax.rem(index, size_y)
                here = terms_ref[z, y, to, core, upper].astype(jnp.float32)
                there = pair_ref[z, y, to, upper].astype(jnp.float32)
                pair_ref[z, y, to, upper] = (here + there).astype(jnp.bfloat16)
        else:
            to = near(size_y, at_y, step)

            @pl.loop(0, size_z * size_x)
            def _(index):
                z, x = index // size_x, lax.rem(index, size_x)
                here = terms_ref[z, to, x, core, lower].astype(jnp.float32)
                there = pair_ref[z, to, x, lower].astype(jnp.float32)
                pair_ref[z, to, x, lower] = (here + there).astype(jnp.bfloat16)

    second_x, second_y = [], []
    for copy, (way, step) in zip(pairs, pieces):
        copy.wait_recv()
        add_pair(way, step)
        if step and way == "x":
            source = pair_ref.at[:, :, near(size_x, at_x, step), upper]
            second_x.append(send(source, upper_two.at[step - 1], 2, step))
        elif step:
            source = pair_ref.at[:, near(size_y, at_y, step), :, lower]
            second_y.append(send(source, lower_two.at[step - 1], 1, step))

    for copy in second_x:
        copy.wait_recv()
    third_y, third_x = [], []
    for step in list(range(1, size_y)) + [0]:
        to = near(size_y, at_y, step)

        @pl.loop(0, size_z)
        def _(z):
            total = pair_ref[z, to, at_x, upper].astype(jnp.float32)
            for index in range(size_x - 1):
                total += upper_two[index, z, to].astype(jnp.float32)
            pair_ref[z, to, at_x, upper] = total.astype(jnp.bfloat16)

        if step:
            source = pair_ref.at[:, to, at_x, upper]
            third_y.append(send(source, upper_three.at[step - 1], 1, step))
    for copy in second_y:
        copy.wait_recv()
    for step in list(range(1, size_x)) + [0]:
        to = near(size_x, at_x, step)

        @pl.loop(0, size_z)
        def _(z):
            total = pair_ref[z, at_y, to, lower].astype(jnp.float32)
            for index in range(size_y - 1):
                total += lower_two[index, z, to].astype(jnp.float32)
            pair_ref[z, at_y, to, lower] = total.astype(jnp.bfloat16)

        if step:
            source = pair_ref.at[:, at_y, to, lower]
            third_x.append(send(source, lower_three.at[step - 1], 2, step))

    last = []
    for band, third, arrived, count in (
        (upper, third_y, upper_three, size_y - 1),
        (lower, third_x, lower_three, size_x - 1),
    ):
        for copy in third:
            copy.wait_recv()
        for step in list(range(1, size_z)) + [0]:
            to = near(size_z, at_z, step)
            total = pair_ref[to, at_y, at_x, band].astype(jnp.float32)
            for index in range(count):
                total += arrived[index, to].astype(jnp.float32)
            if step:
                pair_ref[to, at_y, at_x, band] = total.astype(jnp.bfloat16)
                source = pair_ref.at[to, at_y, at_x, band]
                last.append(send(source, last_ref.at[step - 1, band], 0, step))
            else:
                out_ref[band] = total
    for copy in last:
        copy.wait_recv()
    for index in range(size_z - 1):
        out_ref[...] += last_ref[index].astype(jnp.float32)
    for copy in pairs + links:
        copy.wait_send()


def scatter_sum(terms, sizes):
    rows = terms.shape[-2]
    cut = (rows // ROW_TILE + 1) // 2 * ROW_TILE
    rest = rows - cut
    size_z, size_y, size_x = sizes[:3]
    core_count = size_x + size_y
    link_count = 2 * (sizes[0] - 1) + 2 * (sizes[1] - 1) + 2 * (sizes[2] - 1)
    scratch = lambda *shape: pltpu.VMEM(shape + (LANES,), jnp.bfloat16)
    return pl.pallas_call(
        functools.partial(scatter_kernel, sizes, cut),
        out_shape=jax.ShapeDtypeStruct((rows, LANES), jnp.float32),
        in_specs=[pl.BlockSpec(memory_space=pltpu.VMEM)],
        out_specs=pl.BlockSpec(memory_space=pltpu.VMEM),
        scratch_shapes=[
            scratch(size_z, size_y, size_x, rows),
            scratch(size_x - 1, size_z, size_y, cut),
            scratch(size_y - 1, size_z, size_x, rest),
            scratch(size_y - 1, size_z, cut),
            scratch(size_x - 1, size_z, rest),
            scratch(size_z - 1, rows),
            pltpu.SemaphoreType.DMA((core_count,)),
            pltpu.SemaphoreType.DMA((core_count,)),
            pltpu.SemaphoreType.DMA((link_count,)),
            pltpu.SemaphoreType.DMA((link_count,)),
        ],
        compiler_params=pltpu.CompilerParams(
            collective_id=1, has_side_effects=True, vmem_limit_bytes=40 * 1024 * 1024
        ),
    )(terms)


def pack_rows(pieces, axis):
    joined = jnp.concatenate(pieces, axis=axis)
    length = joined.shape[-1]
    block = ROW_TILE * LANES
    extra = -length % block
    if extra:
        pad = [(0, 0)] * (joined.ndim - 1) + [(0, extra)]
        joined = jnp.pad(joined, pad)
    return joined.reshape(joined.shape[:-1] + (-1, LANES))


def per_device(
    latents,
    condition,
    modulation_weight,
    input_weight,
    output_weight,
    first_weight,
    second_weight,
    all_biases,
    cotangent,
):
    model_width = latents.shape[-1]
    devices = lax.axis_size("fsdp")
    sizes = slice_shape(devices)
    shards = (
        modulation_weight,
        input_weight,
        output_weight,
        first_weight,
        second_weight,
        all_biases,
    )
    gathered = gather_all(pack_rows(shards, 0), sizes)
    gathered = gathered.reshape(devices, -1, LANES)
    flat, start = [], 0
    aligned = all(shard.shape[0] % LANES == 0 for shard in shards[:-1])
    for shard in shards:
        length = shard.shape[0]
        if aligned:
            first_row, row_count = start // LANES, -(-length // LANES)
            part = gathered[:, first_row : first_row + row_count].reshape(devices, -1)
            flat.append(part[:, :length].reshape(-1))
        else:
            part = gathered.reshape(devices, -1)[:, start : start + length]
            flat.append(part.reshape(-1))
        start += length
    params = unpack(*flat, model_width, FF)
    block_output, saved_state = forward_pass(latents, condition, params, batched)
    grad_middle, mods_two, grad_first, grad_second, bias_first, bias_second = backward_feed(
        cotangent, saved_state, params
    )
    grad_latents, grad_condition, grad_modw, grad_inproj, grad_outproj, biases_head = (
        backward_attention(grad_middle, mods_two, saved_state, params, batched)
    )
    bias_vector = jnp.concatenate(
        [biases_head[0], biases_head[1], biases_head[2], biases_head[3], bias_first, bias_second]
    )
    terms = (grad_modw, grad_inproj, grad_outproj, grad_first, grad_second, bias_vector)
    terms = [term.astype(jnp.bfloat16).reshape(devices, -1) for term in terms]
    packed = pack_rows(terms, 1)
    summed = scatter_sum(packed.reshape(tuple(sizes) + packed.shape[1:]), sizes).reshape(-1)
    sums, start = [], 0
    for shard in shards:
        sums.append(summed[start : start + shard.shape[0]])
        start += shard.shape[0]
    return (
        block_output,
        grad_latents,
        grad_condition,
        *sums,
    )


def solution(mesh):
    in_specs = (
        P("fsdp", None, None),
        P("fsdp", None),
        P("fsdp"),
        P("fsdp"),
        P("fsdp"),
        P("fsdp"),
        P("fsdp"),
        P("fsdp"),
        P("fsdp", None, None),
    )
    out_specs = (
        P("fsdp", None, None),
        P("fsdp", None, None),
        P("fsdp", None),
        P("fsdp"),
        P("fsdp"),
        P("fsdp"),
        P("fsdp"),
        P("fsdp"),
        P("fsdp"),
    )
    return jax.shard_map(
        per_device, mesh=mesh, in_specs=in_specs, out_specs=out_specs, check_vma=False
    )
```

```python
import functools
import math

import jax
import jax.numpy as jnp
from jax import lax
from jax.experimental import pallas as pl
from jax.experimental.pallas import tpu as pltpu
from jax.sharding import PartitionSpec as P

HEADS = 6
HDIM = 64
FF = 1536


EPSILON = 1e-06


def product(left, right):
    return jnp.dot(left, right, preferred_element_type=jnp.float32)


def normalize(inputs):
    average = jnp.mean(inputs, axis=-1, keepdims=True)
    centered = inputs - average
    inv_std = lax.rsqrt(jnp.mean(centered * centered, axis=-1, keepdims=True) + EPSILON)
    return (centered * inv_std, inv_std)


def normalize_back(grad_normed, normed, inv_std):
    first_mean = jnp.mean(grad_normed, axis=-1, keepdims=True)
    second_mean = jnp.mean(grad_normed * normed, axis=-1, keepdims=True)
    return inv_std * (grad_normed - first_mean - normed * second_mean)


def unpack(
    flat_mod, flat_input, flat_output, flat_first, flat_second, bias_flat, model_width, hidden
):
    bias_float = bias_flat.astype(jnp.float32)
    return {
        "mod": flat_mod.reshape(model_width, 6 * model_width),
        "inproj": flat_input.reshape(model_width, 3 * model_width),
        "outproj": flat_output.reshape(model_width, model_width),
        "first": flat_first.reshape(model_width, hidden),
        "second": flat_second.reshape(hidden, model_width),
        "bias_mod": bias_float[: 6 * model_width],
        "bias_query": bias_float[6 * model_width : 7 * model_width],
        "bias_value": bias_float[7 * model_width : 8 * model_width],
        "bias_outproj": bias_float[8 * model_width : 9 * model_width],
        "bias_first": bias_float[9 * model_width : 9 * model_width + hidden],
        "bias_second": bias_float[9 * model_width + hidden :],
    }


def contract(left, right, left_dim, right_dim):
    return lax.dot_general(
        left,
        right,
        (((left_dim,), (right_dim,)), ((), ())),
        preferred_element_type=jnp.float32,
    )


def token_sum(values):
    return jnp.sum(values, axis=0, keepdims=True)


def gelu_parts(inputs):
    scale = math.sqrt(2.0 / math.pi)
    square = inputs * inputs
    curve = jnp.tanh(scale * inputs * (1.0 + 0.044715 * square))
    half = 0.5 * (1.0 + curve)
    inner = scale * (1.0 + 3.0 * 0.044715 * square)
    return inputs * half, half + 0.5 * inputs * (1.0 - curve * curve) * inner


def block_kernel(
    lat_ref,
    cot_ref,
    mod_ref,
    win_ref,
    wout_ref,
    wfirst_ref,
    wsecond_ref,
    bias_ref,
    bfirst_ref,
    out_ref,
    glat_ref,
    gmod_ref,
    gin_ref,
    gout_ref,
    gfirst_ref,
    gsecond_ref,
    gbias_ref,
    gbfirst_ref,
    acc_in,
    acc_out,
    acc_first,
    acc_second,
    prob_ref,
    slope_ref,
    act_ref,
):
    step = pl.program_id(0)
    width = lat_ref.shape[-1]
    hidden = wfirst_ref.shape[1]
    chunk = hidden // 3
    score_scale = 1.0 / math.sqrt(HDIM)
    pair = 2 * HDIM

    @pl.when(step == 0)
    def _():
        for ref in (acc_in, acc_out, acc_first, acc_second, gbias_ref, gbfirst_ref):
            ref[...] = jnp.zeros_like(ref)

    shift_one, scale_one, gate_one, shift_two, scale_two, gate_two = [
        mod_ref[0, index : index + 1, :] for index in range(6)
    ]
    bias_query, bias_value, bias_out, bias_second = [
        bias_ref[index : index + 1, :] for index in range(4)
    ]
    inputs = lat_ref[0].astype(jnp.float32)
    normed_one, inv_one = normalize(inputs)
    modul_one = (normed_one * (1.0 + scale_one) + shift_one).astype(jnp.bfloat16)
    queries = (product(modul_one, win_ref[:, :width]) + bias_query).astype(jnp.bfloat16)
    keys = product(modul_one, win_ref[:, width : 2 * width]).astype(jnp.bfloat16)
    values = (product(modul_one, win_ref[:, 2 * width :]) + bias_value).astype(jnp.bfloat16)

    tokens = inputs.shape[0]
    lane = lax.broadcasted_iota(jnp.int32, (tokens, pair), 1)
    sides = (lane < HDIM, lane >= HDIM)

    def side(pair_values, which):
        return jnp.where(sides[which], pair_values, jnp.zeros_like(pair_values))

    attended = []
    for index in range(width // pair):
        cols = slice(index * pair, (index + 1) * pair)
        total = None
        for which in range(2):
            scores = contract(side(queries[:, cols], which), keys[:, cols], 1, 1) * score_scale
            raised = jnp.exp(scores - jnp.max(scores, axis=-1, keepdims=True))
            probs = raised * (1.0 / jnp.sum(raised, axis=-1, keepdims=True))
            prob_ref[2 * index + which] = probs
            part = product(probs.astype(jnp.bfloat16), side(values[:, cols], which))
            total = part if total is None else total + part
        attended.append(total.astype(jnp.bfloat16))
    attended = jnp.concatenate(attended, axis=-1)

    branch_one = product(attended, wout_ref[...]) + bias_out
    middle = inputs + gate_one * branch_one
    normed_two, inv_two = normalize(middle)
    modul_two = (normed_two * (1.0 + scale_two) + shift_two).astype(jnp.bfloat16)
    branch_two = bias_second
    for start in range(0, hidden, chunk):
        cols = slice(start, start + chunk)
        pre_act = product(modul_two, wfirst_ref[:, cols]) + bfirst_ref[:, cols]
        active, slope = gelu_parts(pre_act)
        act_ref[:, cols] = active.astype(jnp.bfloat16)
        slope_ref[:, cols] = slope
        branch_two = branch_two + product(active.astype(jnp.bfloat16), wsecond_ref[cols, :])
    out_ref[0] = (middle + gate_two * branch_two).astype(jnp.bfloat16)

    upstream = cot_ref[0].astype(jnp.float32)
    gmod_ref[0, 5:6, :] = token_sum(upstream * branch_two)
    grad_branch = upstream * gate_two
    branch_round = grad_branch.astype(jnp.bfloat16)
    gbias_ref[3:4, :] += token_sum(grad_branch)
    modul_turned = modul_two.T
    grad_modul = None
    for start in range(0, hidden, chunk):
        cols = slice(start, start + chunk)
        acc_second[cols, :] += contract(act_ref[:, cols], branch_round, 0, 0)
        grad_pre = contract(branch_round, wsecond_ref[cols, :], 1, 1) * slope_ref[:, cols]
        gbfirst_ref[:, cols] += token_sum(grad_pre)
        pre_round = grad_pre.astype(jnp.bfloat16)
        acc_first[:, cols] += product(modul_turned, pre_round)
        part = contract(pre_round, wfirst_ref[:, cols], 1, 1)
        grad_modul = part if grad_modul is None else grad_modul + part
    gmod_ref[0, 3:4, :] = token_sum(grad_modul)
    gmod_ref[0, 4:5, :] = token_sum(grad_modul * normed_two)
    grad_middle = upstream + normalize_back(grad_modul * (1.0 + scale_two), normed_two, inv_two)

    gmod_ref[0, 2:3, :] = token_sum(grad_middle * branch_one)
    grad_branch = grad_middle * gate_one
    branch_round = grad_branch.astype(jnp.bfloat16)
    gbias_ref[2:3, :] += token_sum(grad_branch)
    acc_out[...] += contract(attended, branch_round, 0, 0)
    grad_attended = contract(branch_round, wout_ref[...], 1, 1).astype(jnp.bfloat16)

    grad_query, grad_key, grad_value = [], [], []
    for index in range(width // pair):
        cols = slice(index * pair, (index + 1) * pair)
        pair_query, pair_key, pair_value = None, None, None
        for which in range(2):
            probs = prob_ref[2 * index + which]
            attended_side = side(grad_attended[:, cols], which)
            grad_probs = contract(attended_side, values[:, cols], 1, 1)
            row_dots = jnp.sum(probs * grad_probs, axis=-1, keepdims=True)
            grad_scores = (probs * (grad_probs - row_dots) * score_scale).astype(jnp.bfloat16)
            part_query = product(grad_scores, side(keys[:, cols], which))
            part_key = contract(grad_scores, side(queries[:, cols], which), 0, 0)
            part_value = contract(probs.astype(jnp.bfloat16), attended_side, 0, 0)
            if which == 0:
                pair_query, pair_key, pair_value = part_query, part_key, part_value
            else:
                pair_query = pair_query + part_query
                pair_key = pair_key + part_key
                pair_value = pair_value + part_value
        gbias_ref[0:1, cols] += token_sum(pair_query)
        gbias_ref[1:2, cols] += token_sum(pair_value)
        grad_query.append(pair_query.astype(jnp.bfloat16))
        grad_key.append(pair_key.astype(jnp.bfloat16))
        grad_value.append(pair_value.astype(jnp.bfloat16))
    grad_proj = jnp.concatenate(grad_query + grad_key + grad_value, axis=-1)
    acc_in[...] += contract(modul_one, grad_proj, 0, 0)
    grad_modul = contract(grad_proj, win_ref[...], 1, 1)
    gmod_ref[0, 0:1, :] = token_sum(grad_modul)
    gmod_ref[0, 1:2, :] = token_sum(grad_modul * normed_one)
    glat_ref[0] = grad_middle + normalize_back(
        grad_modul * (1.0 + scale_one), normed_one, inv_one
    )

    @pl.when(step == pl.num_programs(0) - 1)
    def _():
        gin_ref[...] = acc_in[...].astype(jnp.bfloat16)
        gout_ref[...] = acc_out[...].astype(jnp.bfloat16)
        gfirst_ref[...] = acc_first[...].astype(jnp.bfloat16)
        gsecond_ref[...] = acc_second[...].astype(jnp.bfloat16)


def run_block(latents, cotangent, mods, params):
    count, tokens, width = latents.shape
    hidden = params["first"].shape[1]
    biases = jnp.stack(
        [
            params["bias_query"],
            params["bias_value"],
            params["bias_outproj"],
            params["bias_second"],
        ]
    )
    once = lambda *shape: pl.BlockSpec(
        shape, lambda step: (0,) * len(shape), pipeline_mode=pl.Buffered(1)
    )
    each = lambda *shape: pl.BlockSpec((1,) + shape, lambda step: (step, 0, 0))
    weights = [(width, 3 * width), (width, width), (width, hidden), (hidden, width)]
    like = jax.ShapeDtypeStruct
    return pl.pallas_call(
        block_kernel,
        grid=(count,),
        in_specs=[each(tokens, width), each(tokens, width), each(6, width)]
        + [once(*shape) for shape in weights]
        + [once(4, width), once(1, hidden)],
        out_specs=[each(tokens, width), each(tokens, width), each(6, width)]
        + [once(*shape) for shape in weights]
        + [once(4, width), once(1, hidden)],
        out_shape=[
            like(latents.shape, jnp.bfloat16),
            like(latents.shape, jnp.float32),
            like((count, 6, width), jnp.float32),
        ]
        + [like(shape, jnp.bfloat16) for shape in weights]
        + [like((4, width), jnp.float32), like((1, hidden), jnp.float32)],
        scratch_shapes=[pltpu.VMEM(shape, jnp.float32) for shape in weights]
        + [
            pltpu.VMEM((HEADS, tokens, tokens), jnp.float32),
            pltpu.VMEM((tokens, hidden), jnp.float32),
            pltpu.VMEM((tokens, hidden), jnp.bfloat16),
        ],
        compiler_params=pltpu.CompilerParams(vmem_limit_bytes=56 * 1024 * 1024),
    )(
        latents,
        cotangent,
        mods,
        params["inproj"],
        params["outproj"],
        params["first"],
        params["second"],
        biases,
        params["bias_first"].reshape(1, hidden),
    )


MESH = pl.DeviceIdType.MESH
LANES = 128
ROW_TILE = 16


def slice_shape(devices):
    chips = devices // 2
    edge = 1
    while (2 * edge) ** 3 <= chips:
        edge *= 2
    return (chips // (edge * edge), edge, edge, 2)


def position(sizes):
    size_z, size_y, size_x, size_c = sizes
    me = lax.axis_index("fsdp")
    core = lax.rem(me, size_c)
    chip = me // size_c
    at_x = lax.rem(chip, size_x)
    at_y = lax.rem(chip // size_x, size_y)
    at_z = chip // (size_x * size_y)
    return (at_z, at_y, at_x, core)


def device_at(sizes, at):
    return ((at[0] * sizes[1] + at[1]) * sizes[2] + at[2]) * sizes[3] + at[3]


def moved(sizes, at, axis, step):
    at = list(at)
    at[axis] = lax.rem(at[axis] + step, sizes[axis])
    return tuple(at)


def enter(sizes, at):
    barrier = pltpu.get_barrier_semaphore()
    total = 0
    for axis in range(4):
        for step in range(1, sizes[axis]):
            peer = device_at(sizes, moved(sizes, at, axis, step))
            pl.semaphore_signal(barrier, inc=1, device_id=(peer,), device_id_type=MESH)
            total += 1
    pl.semaphore_wait(barrier, total)


def gather_kernel(sizes, cut, shard_ref, full_ref, own_sem, send_sem, recv_sem, core_send, core_recv):
    at = position(sizes)
    at_z, at_y, at_x, core = at
    rows = shard_ref.shape[0]
    upper, lower = pl.ds(0, cut), pl.ds(cut, rows - cut)
    enter(sizes, at)
    links, cores = [], []

    def send(source, target, axis, step):
        slot = len(links)
        copy = pltpu.make_async_remote_copy(
            src_ref=source,
            dst_ref=target,
            send_sem=send_sem.at[slot],
            recv_sem=recv_sem.at[slot],
            device_id=(device_at(sizes, moved(sizes, at, axis, step)),),
            device_id_type=MESH,
        )
        copy.start()
        links.append(copy)
        return copy

    def share(source, target):
        slot = len(cores)
        copy = pltpu.make_async_remote_copy(
            src_ref=source,
            dst_ref=target,
            send_sem=core_send.at[slot],
            recv_sem=core_recv.at[slot],
            device_id=(device_at(sizes, moved(sizes, at, 3, 1)),),
            device_id_type=MESH,
        )
        copy.start()
        cores.append(copy)

    mine = full_ref.at[at_z, at_y, at_x, core]
    first = [send(shard_ref, mine, 0, step) for step in range(1, sizes[0])]
    share(shard_ref, mine)
    own = pltpu.make_async_copy(shard_ref, mine, own_sem)
    own.start()
    own.wait()
    for copy in first:
        copy.wait_recv()
    along_y, along_x = [], []
    column = full_ref.at[:, at_y, at_x, core, upper]
    for step in range(1, sizes[1]):
        along_y.append(send(column, column, 1, step))
    column = full_ref.at[:, at_y, at_x, core, lower]
    for step in range(1, sizes[2]):
        along_x.append(send(column, column, 2, step))
    for step in range(1, sizes[0]):
        piece = full_ref.at[lax.rem(at_z + sizes[0] - step, sizes[0]), at_y, at_x, core]
        share(piece, piece)
    for copy in along_y:
        copy.wait_recv()
    last_x, last_y = [], []
    plane = full_ref.at[:, :, at_x, core, upper]
    for step in range(1, sizes[2]):
        last_x.append(send(plane, plane, 2, step))
    for copy in along_x:
        copy.wait_recv()
    plane = full_ref.at[:, at_y, :, core, lower]
    for step in range(1, sizes[1]):
        last_y.append(send(plane, plane, 1, step))
    for step in range(1, sizes[1]):
        piece = full_ref.at[:, lax.rem(at_y + sizes[1] - step, sizes[1]), at_x, core, upper]
        share(piece, piece)
    for step in range(1, sizes[2]):
        piece = full_ref.at[:, at_y, lax.rem(at_x + sizes[2] - step, sizes[2]), core, lower]
        share(piece, piece)
    for step, copy in enumerate(last_x, 1):
        copy.wait_recv()
        piece = full_ref.at[:, :, lax.rem(at_x + sizes[2] - step, sizes[2]), core, upper]
        share(piece, piece)
    for step, copy in enumerate(last_y, 1):
        copy.wait_recv()
        piece = full_ref.at[:, lax.rem(at_y + sizes[1] - step, sizes[1]), :, core, lower]
        share(piece, piece)
    for copy in links:
        copy.wait_send()
    for copy in cores:
        copy.wait()


def gather_all(shard, sizes):
    rows = shard.shape[0]
    cut = (rows // ROW_TILE + 1) // 2 * ROW_TILE
    link_count = (sizes[0] - 1) + 2 * (sizes[1] - 1) + 2 * (sizes[2] - 1)
    core_count = link_count + 1
    return pl.pallas_call(
        functools.partial(gather_kernel, sizes, cut),
        out_shape=jax.ShapeDtypeStruct(tuple(sizes) + shard.shape, shard.dtype),
        in_specs=[pl.BlockSpec(memory_space=pl.ANY)],
        out_specs=pl.BlockSpec(memory_space=pl.ANY),
        scratch_shapes=[
            pltpu.SemaphoreType.DMA,
            pltpu.SemaphoreType.DMA((link_count,)),
            pltpu.SemaphoreType.DMA((link_count,)),
            pltpu.SemaphoreType.DMA((core_count,)),
            pltpu.SemaphoreType.DMA((core_count,)),
        ],
        compiler_params=pltpu.CompilerParams(collective_id=0, has_side_effects=True),
    )(shard)


def scatter_kernel(
    sizes,
    cut,
    terms_ref,
    out_ref,
    pair_ref,
    upper_two,
    lower_two,
    upper_three,
    lower_three,
    last_ref,
    core_send,
    core_recv,
    send_sem,
    recv_sem,
):
    size_z, size_y, size_x = sizes[:3]
    at = position(sizes)
    at_z, at_y, at_x, core = at
    rows = out_ref.shape[0]
    upper, lower = pl.ds(0, cut), pl.ds(cut, rows - cut)
    links = []
    enter(sizes, at)

    def send(source, target, axis, step):
        slot = len(links)
        copy = pltpu.make_async_remote_copy(
            src_ref=source,
            dst_ref=target,
            send_sem=send_sem.at[slot],
            recv_sem=recv_sem.at[slot],
            device_id=(device_at(sizes, moved(sizes, at, axis, step)),),
            device_id_type=MESH,
        )
        copy.start()
        links.append(copy)
        return copy

    def near(size, place, step):
        return lax.rem(place + step, size)

    other = 1 - core
    pairs = []
    pieces = [("x", step) for step in range(1, size_x)] + [("y", step) for step in range(1, size_y)]
    pieces += [("x", 0), ("y", 0)]
    for slot, (way, step) in enumerate(pieces):
        if way == "x":
            to = near(size_x, at_x, step)
            source = terms_ref.at[:, :, to, other, upper]
            target = pair_ref.at[:, :, to, upper]
        else:
            to = near(size_y, at_y, step)
            source = terms_ref.at[:, to, :, other, lower]
            target = pair_ref.at[:, to, :, lower]
        copy = pltpu.make_async_remote_copy(
            src_ref=source,
            dst_ref=target,
            send_sem=core_send.at[slot],
            recv_sem=core_recv.at[slot],
            device_id=(device_at(sizes, moved(sizes, at, 3, 1)),),
            device_id_type=MESH,
        )
        copy.start()
        pairs.append(copy)

    def add_pair(way, step):
        if way == "x":
            to = near(size_x, at_x, step)

            @pl.loop(0, size_z * size_y)
            def _(index):
                z, y = index // size_y, lax.rem(index, size_y)
                here = terms_ref[z, y, to, core, upper].astype(jnp.float32)
                there = pair_ref[z, y, to, upper].astype(jnp.float32)
                pair_ref[z, y, to, upper] = (here + there).astype(jnp.bfloat16)
        else:
            to = near(size_y, at_y, step)

            @pl.loop(0, size_z * size_x)
            def _(index):
                z, x = index // size_x, lax.rem(index, size_x)
                here = terms_ref[z, to, x, core, lower].astype(jnp.float32)
                there = pair_ref[z, to, x, lower].astype(jnp.float32)
                pair_ref[z, to, x, lower] = (here + there).astype(jnp.bfloat16)

    second_x, second_y = [], []
    for copy, (way, step) in zip(pairs, pieces):
        copy.wait_recv()
        add_pair(way, step)
        if step and way == "x":
            source = pair_ref.at[:, :, near(size_x, at_x, step), upper]
            second_x.append(send(source, upper_two.at[step - 1], 2, step))
        elif step:
            source = pair_ref.at[:, near(size_y, at_y, step), :, lower]
            second_y.append(send(source, lower_two.at[step - 1], 1, step))

    for copy in second_x:
        copy.wait_recv()
    third_y, third_x = [], []
    for step in list(range(1, size_y)) + [0]:
        to = near(size_y, at_y, step)

        @pl.loop(0, size_z)
        def _(z):
            total = pair_ref[z, to, at_x, upper].astype(jnp.float32)
            for index in range(size_x - 1):
                total += upper_two[index, z, to].astype(jnp.float32)
            pair_ref[z, to, at_x, upper] = total.astype(jnp.bfloat16)

        if step:
            source = pair_ref.at[:, to, at_x, upper]
            third_y.append(send(source, upper_three.at[step - 1], 1, step))
    for copy in second_y:
        copy.wait_recv()
    for step in list(range(1, size_x)) + [0]:
        to = near(size_x, at_x, step)

        @pl.loop(0, size_z)
        def _(z):
            total = pair_ref[z, at_y, to, lower].astype(jnp.float32)
            for index in range(size_y - 1):
                total += lower_two[index, z, to].astype(jnp.float32)
            pair_ref[z, at_y, to, lower] = total.astype(jnp.bfloat16)

        if step:
            source = pair_ref.at[:, at_y, to, lower]
            third_x.append(send(source, lower_three.at[step - 1], 2, step))

    last = []
    for band, third, arrived, count in (
        (upper, third_y, upper_three, size_y - 1),
        (lower, third_x, lower_three, size_x - 1),
    ):
        for copy in third:
            copy.wait_recv()
        for step in list(range(1, size_z)) + [0]:
            to = near(size_z, at_z, step)
            total = pair_ref[to, at_y, at_x, band].astype(jnp.float32)
            for index in range(count):
                total += arrived[index, to].astype(jnp.float32)
            if step:
                pair_ref[to, at_y, at_x, band] = total.astype(jnp.bfloat16)
                source = pair_ref.at[to, at_y, at_x, band]
                last.append(send(source, last_ref.at[step - 1, band], 0, step))
            else:
                out_ref[band] = total
    for copy in last:
        copy.wait_recv()
    for index in range(size_z - 1):
        out_ref[...] += last_ref[index].astype(jnp.float32)
    for copy in pairs + links:
        copy.wait_send()


def scatter_sum(terms, sizes):
    rows = terms.shape[-2]
    cut = (rows // ROW_TILE + 1) // 2 * ROW_TILE
    rest = rows - cut
    size_z, size_y, size_x = sizes[:3]
    core_count = size_x + size_y
    link_count = 2 * (sizes[0] - 1) + 2 * (sizes[1] - 1) + 2 * (sizes[2] - 1)
    scratch = lambda *shape: pltpu.VMEM(shape + (LANES,), jnp.bfloat16)
    return pl.pallas_call(
        functools.partial(scatter_kernel, sizes, cut),
        out_shape=jax.ShapeDtypeStruct((rows, LANES), jnp.float32),
        in_specs=[pl.BlockSpec(memory_space=pltpu.VMEM)],
        out_specs=pl.BlockSpec(memory_space=pltpu.VMEM),
        scratch_shapes=[
            scratch(size_z, size_y, size_x, rows),
            scratch(size_x - 1, size_z, size_y, cut),
            scratch(size_y - 1, size_z, size_x, rest),
            scratch(size_y - 1, size_z, cut),
            scratch(size_x - 1, size_z, rest),
            scratch(size_z - 1, rows),
            pltpu.SemaphoreType.DMA((core_count,)),
            pltpu.SemaphoreType.DMA((core_count,)),
            pltpu.SemaphoreType.DMA((link_count,)),
            pltpu.SemaphoreType.DMA((link_count,)),
        ],
        compiler_params=pltpu.CompilerParams(
            collective_id=1, has_side_effects=True, vmem_limit_bytes=40 * 1024 * 1024
        ),
    )(terms)


def pack_rows(pieces, axis):
    joined = jnp.concatenate(pieces, axis=axis)
    length = joined.shape[-1]
    block = ROW_TILE * LANES
    extra = -length % block
    if extra:
        pad = [(0, 0)] * (joined.ndim - 1) + [(0, extra)]
        joined = jnp.pad(joined, pad)
    return joined.reshape(joined.shape[:-1] + (-1, LANES))


def per_device(
    latents,
    condition,
    modulation_weight,
    input_weight,
    output_weight,
    first_weight,
    second_weight,
    all_biases,
    cotangent,
):
    model_width = latents.shape[-1]
    devices = lax.axis_size("fsdp")
    sizes = slice_shape(devices)
    shards = (
        modulation_weight,
        input_weight,
        output_weight,
        first_weight,
        second_weight,
        all_biases,
    )
    gathered = gather_all(pack_rows(shards, 0), sizes)
    gathered = gathered.reshape(devices, -1, LANES)
    flat, start = [], 0
    aligned = all(shard.shape[0] % LANES == 0 for shard in shards[:-1])
    for shard in shards:
        length = shard.shape[0]
        if aligned:
            first_row, row_count = start // LANES, -(-length // LANES)
            part = gathered[:, first_row : first_row + row_count].reshape(devices, -1)
            flat.append(part[:, :length].reshape(-1))
        else:
            part = gathered.reshape(devices, -1)[:, start : start + length]
            flat.append(part.reshape(-1))
        start += length
    params = unpack(*flat, model_width, FF)
    cond_float = condition.astype(jnp.float32)
    cond_act = jax.nn.silu(cond_float).astype(jnp.bfloat16)
    mods = product(cond_act, params["mod"]) + params["bias_mod"]
    (
        block_output,
        grad_latents,
        grad_mod,
        grad_inproj,
        grad_outproj,
        grad_first,
        grad_second,
        grad_bias,
        bias_first,
    ) = run_block(latents, cotangent, mods.reshape(-1, 6, model_width), params)
    grad_mod = grad_mod.reshape(-1, 6 * model_width)
    mod_round = grad_mod.astype(jnp.bfloat16)
    grad_modw = product(cond_act.T, mod_round)
    grad_cond_act = product(mod_round, params["mod"].T)
    grad_condition = jax.vjp(jax.nn.silu, cond_float)[1](grad_cond_act)[0]
    bias_vector = jnp.concatenate(
        [
            jnp.sum(grad_mod, axis=0),
            grad_bias[0],
            grad_bias[1],
            grad_bias[2],
            bias_first[0],
            grad_bias[3],
        ]
    )
    terms = (grad_modw, grad_inproj, grad_outproj, grad_first, grad_second, bias_vector)
    terms = [term.astype(jnp.bfloat16).reshape(devices, -1) for term in terms]
    packed = pack_rows(terms, 1)
    summed = scatter_sum(packed.reshape(tuple(sizes) + packed.shape[1:]), sizes).reshape(-1)
    sums, start = [], 0
    for shard in shards:
        sums.append(summed[start : start + shard.shape[0]])
        start += shard.shape[0]
    return (
        block_output,
        grad_latents,
        grad_condition,
        *sums,
    )


def solution(mesh):
    in_specs = (
        P("fsdp", None, None),
        P("fsdp", None),
        P("fsdp"),
        P("fsdp"),
        P("fsdp"),
        P("fsdp"),
        P("fsdp"),
        P("fsdp"),
        P("fsdp", None, None),
    )
    out_specs = (
        P("fsdp", None, None),
        P("fsdp", None, None),
        P("fsdp", None),
        P("fsdp"),
        P("fsdp"),
        P("fsdp"),
        P("fsdp"),
        P("fsdp"),
        P("fsdp"),
    )
    return jax.shard_map(
        per_device, mesh=mesh, in_specs=in_specs, out_specs=out_specs, check_vma=False
    )
```
